256 devices in a mesh: grp: 8 (over y, z_lo), dev: 32 (over x, z_hi, core).
Axes of the slice: x: 4, y: 4, z: 8 (z_hi: 4, z_lo: 2; z = z_hi * 2 + z_lo), core: 2. Of those that a mesh axis runs over, the one named last changes fastest.
Arguments:
- resid: bfloat16 [32768, 1536], P(('grp', 'dev')), may hold values from -1.5 to 1.5
- queries: bfloat16 [32768, 1536], P(('grp', 'dev')), may hold values from -6 to 6
- suffix_kv: bfloat16 [32768, 2, 512], P(('grp', 'dev')), may hold values from -6 to 6
- prefix_kv: bfloat16 [8, 2048, 2, 512], P('grp', 'dev'), may hold values from -6 to 6
- segments: int32 [256, 128], P(('grp', 'dev')), may hold values from 0 to 3, never falling along the last dimension, each value on 1 to 64 neighbouring positions
- o_weight: bfloat16 [1536, 1536], P(('grp', 'dev')), may hold values from -0.15625 to 0.15625
- norm_gain: float32 [1536], replicated, may hold values from 0.25 to 1.75
- router: bfloat16 [1536, 32], replicated, may hold values from -0.15625 to 0.15625
- routes: int32 [32768, 8], P(('grp', 'dev')), may hold values from 0 to 31, all different within a row; in each aligned block of 128 rows (0 to 127, 128 to 255, ...) at most 48 rows name the same one
- w_gate_up: bfloat16 [32, 1536, 1024], P('dev', 'grp'), may hold values from -0.15625 to 0.15625
- w_down: bfloat16 [32, 512, 1536], P('dev', 'grp'), may hold values from -0.25 to 0.25
Outputs:
- layer_out: bfloat16 [32768, 1536], P(('grp', 'dev'))
The draws below stay inside these ranges and needn't reach their ends.
Inputs may be any that keep to these rules, and one draw needn't show every extreme that they name: At most 48 of one device's routes name one expert.
All inputs are finite; a program needn't handle non-finite values.
Results may differ from the reference program's by a relative error of at most 0.012.
Values may be sent and summed in bfloat16 or wider, within the bound.
A program may use at most 128 MiB of HBM per device.

```python
import math
import jax
import jax.numpy as jnp
import numpy as np
from jax import lax

D = 1536
HEADS = 24
KVH = 8
HDIM = 64
FFE = 512
TOPK = 8
EXPERTS = 32
PREFIX = 2048
REQS = 4
TOK_DEV = 128
ATT = 1536
CAP = 48
GROUPS = 8
BLOCKS = 256
TOKENS = 32768
SEG_MOST = 64
N_GRP = 8
N_DEV = 32


def draw_queries(key, part):
    base = jnp.clip(2.0 * jax.random.normal(jax.random.fold_in(key, 1), (TOKENS, ATT), jnp.float32), -6.0, 6.0)
    return base.astype(jnp.bfloat16)


def draw_prefix_kv(key, part):
    shape = (GROUPS, PREFIX, 2, KVH * HDIM)
    base = jnp.clip(jax.random.normal(jax.random.fold_in(key, 2), shape, jnp.float32), -6.0, 6.0)
    return base.astype(jnp.bfloat16)


def level_of(key, shape, pieces, smallest, top_value):
    def one(position, parts):
        heights = jax.random.uniform(jax.random.fold_in(jax.random.fold_in(key, 6), position), (parts,), jnp.float32, smallest / len(pieces), top_value / len(pieces))
        return jnp.repeat(jnp.exp(heights), shape[position] // parts).reshape((-1,) + (1,) * (len(shape) - position - 1))

    gain = one(*pieces[0])
    for cut in pieces[1:]:
        gain = gain * one(*cut)
    return gain


def length_profile(count, total, bound, skew):
    portions = [(1 << 20) // math.isqrt(rank ** skew) + 1 for rank in range(2, count + 1)]
    surplus, counts = total - bound - (count - 1), [1] * (count - 1)
    while surplus > 0:
        free = [i for i in range(count - 1) if counts[i] < bound]
        mass, budget = sum([portions[i] for i in free]), surplus
        for i in free:
            addition = min(bound - counts[i], max(1, budget * portions[i] // mass), surplus)
            counts[i] = counts[i] + addition
            surplus = surplus - addition
    return np.array([bound] + counts)


def uneven(key, amount, total, most, lean):
    if amount == 2:
        one = jax.random.randint(key, (), max(1, total - most), min(most, total - 1) + 1)
        return jnp.stack([one, total - one])
    tallies = jnp.asarray(length_profile(amount, total, most, lean), jnp.int32)
    pairs = (amount - 1) // 2
    donor, receiver = tallies[1:1 + 2 * pairs:2], tallies[2:2 + 2 * pairs:2]
    room = jnp.minimum(donor - 1, most - receiver)
    moved = jax.random.randint(jax.random.fold_in(key, 1), (pairs,), 0, 1 << 20) % (room + 1)
    tallies = tallies.at[1:1 + 2 * pairs:2].set(donor - moved).at[2:2 + 2 * pairs:2].set(receiver + moved)
    return tallies[jax.random.permutation(jax.random.fold_in(key, 2), amount)]


def routed_block(own_key, own, number, rows, amount, top, reach, lean):
    order = jax.random.permutation(own_key, amount)
    packed, usual = portions_of(amount, rows * top, reach, lean, True), portions_of(amount, rows * top, reach, lean, False)
    places = jnp.arange(amount)

    def named(lengths, offset_by):
        used = int((lengths > 0).sum())
        fixed = max(1, used // 4)
        passed = fixed + (places - fixed + offset_by * (used - fixed)) % max(1, amount - fixed)
        return jnp.zeros((amount,), jnp.int32).at[order[jnp.where(places < fixed, places, passed)]].set(jnp.asarray(lengths, jnp.int32))

    lengths = jnp.where(number % 4 == 0, named(packed, number // 4), named(usual, number - number // 4 - 1))
    mixed = jax.random.permutation(jax.random.fold_in(own, 3), amount)
    donor, sink = mixed[0:amount // 2 * 2:2], mixed[1:amount // 2 * 2:2]
    margin = jnp.minimum(lengths[donor] - 1, reach - lengths[sink]) // 2
    margin = jnp.where((donor == order[0]) | (sink == order[0]) | (lengths[sink] == 0), 0, jnp.maximum(margin, 0))
    passed = jax.random.randint(jax.random.fold_in(own, 4), (amount // 2,), 0, 1 << 20) % (margin + 1)
    lengths = lengths.at[donor].add(-passed).at[sink].add(passed)
    labels = jnp.searchsorted(jnp.cumsum(lengths), jnp.arange(rows * top), side="right").astype(jnp.int32)
    listing = labels.reshape(top, rows).T
    listing = listing[jax.random.permutation(jax.random.fold_in(own, 1), rows)]
    offset_by = jax.random.randint(jax.random.fold_in(own, 2), (rows, 1), 0, top)
    return jnp.take_along_axis(listing, (jnp.arange(top)[None, :] + offset_by) % top, axis=1)


def portions_of(count, total, reach, skew, full):
    loads = [(1 << 20) // math.isqrt(grade ** skew) + 1 for grade in range(1, count + 1)]
    largest = reach if full else min(reach, max(-(-total // count), total * loads[0] // sum(loads)))
    least = 1 if total - largest >= count - 1 else 0
    counts, surplus = [largest] + [least] * (count - 1), total - largest - least * (count - 1)
    while surplus > 0:
        free = [i for i in range(1, count) if counts[i] < largest] or [i for i in range(1, count) if counts[i] < reach]
        mass, remaining = sum([loads[i] for i in free]), surplus
        for i in free:
            more = min(reach - counts[i], max(1, remaining * loads[i] // mass), surplus)
            counts[i] = counts[i] + more
            surplus = surplus - more
    return np.array(counts)


def bell_draw(rng, shape, width, bound, split=(), held_as=jnp.bfloat16):
    values = jax.random.normal(rng, shape, jnp.float32) * width
    if len(split) > 0:
        values = level_of(rng, shape, split, -0.22, 0.18) * values
    return jnp.clip(values, min=-bound, max=bound).astype(held_as)


def setup_inputs(seed: int = 0) -> dict:
    key_list = jax.random.split(jax.random.key(seed), 12)
    resid = bell_draw(key_list[0], (TOKENS, D), 0.25, 1.5, ((0, 256),))
    queries = draw_queries(jax.random.fold_in(key_list[11], 71), 0)
    suffix_kv = bell_draw(key_list[2], (TOKENS, 2, KVH * HDIM), 1.0, 6.0, ((0, 256),))
    prefix_kv = draw_prefix_kv(jax.random.fold_in(key_list[11], 71), 0)
    segments = jax.vmap(lambda own: jnp.searchsorted(jnp.cumsum(uneven(own, REQS, TOK_DEV, SEG_MOST, 2)), jnp.arange(TOK_DEV), side="right"))(jax.random.split(key_list[4], BLOCKS)).reshape((BLOCKS, TOK_DEV)).astype(jnp.int32)
    o_weight = bell_draw(key_list[5], (ATT, D), ATT ** -0.5, 0.15625, ((0, 256),))
    norm_gain = jnp.clip(1.0 + 0.15 * jax.random.normal(key_list[6], (D,), jnp.float32), 0.25, 1.75)
    router = bell_draw(key_list[7], (D, EXPERTS), D ** -0.5, 0.15625)
    routes_keys = jax.random.split(jax.random.fold_in(key_list[8], 1), TOKENS // TOK_DEV)
    routes_turns = jax.random.permutation(jax.random.fold_in(key_list[8], 3), TOKENS // TOK_DEV)
    routes = jax.vmap(lambda own, number: routed_block(jax.random.fold_in(key_list[8], 2), own, number, TOK_DEV, EXPERTS, TOPK, CAP, 2))(routes_keys, routes_turns).reshape((TOKENS, TOPK))
    w_gate_up = bell_draw(key_list[9], (EXPERTS, D, 2 * FFE), D ** -0.5, 0.15625, ((0, 32), (1, 8)))
    w_down = bell_draw(key_list[10], (EXPERTS, FFE, D), FFE ** -0.5, 0.25, ((0, 32), (1, 8)))
    return dict(resid=resid, queries=queries, suffix_kv=suffix_kv, prefix_kv=prefix_kv, segments=segments, o_weight=o_weight, norm_gain=norm_gain, router=router, routes=routes, w_gate_up=w_gate_up, w_down=w_down)


def reference(resid, queries, suffix_kv, prefix_kv, segments, o_weight, norm_gain, router, routes, w_gate_up, w_down):
    blocks = N_GRP * N_DEV
    ratio = HEADS // KVH
    scale = 1.0 / HDIM ** 0.5
    gate_up_full = w_gate_up.astype(jnp.float32)
    down_full = w_down.astype(jnp.float32)
    expert_ids = jnp.arange(EXPERTS, dtype=jnp.int32)
    slot_ids = jnp.arange(EXPERTS * CAP, dtype=jnp.int32)

    def one_block(block):
        start = (block * TOK_DEV).astype(jnp.int32)
        resid_blk = lax.dynamic_slice_in_dim(resid, start, TOK_DEV, 0)
        query_blk = lax.dynamic_slice_in_dim(queries, start, TOK_DEV, 0)
        suffix_blk = lax.dynamic_slice_in_dim(suffix_kv, start, TOK_DEV, 0)
        route_blk = lax.dynamic_slice_in_dim(routes, start, TOK_DEV, 0)
        seg_blk = lax.dynamic_index_in_dim(segments, block, 0, keepdims=False)
        group = (block // N_DEV).astype(jnp.int32)
        prefix_blk = lax.dynamic_index_in_dim(prefix_kv, group, 0, keepdims=False)
        keys = jnp.concatenate([prefix_blk[:, 0], suffix_blk[:, 0]], 0)
        values = jnp.concatenate([prefix_blk[:, 1], suffix_blk[:, 1]], 0)
        query_heads = query_blk.reshape(TOK_DEV, KVH, ratio, HDIM).astype(jnp.float32)
        key_heads = keys.reshape(-1, KVH, HDIM).astype(jnp.float32)
        value_heads = values.reshape(-1, KVH, HDIM).astype(jnp.float32)
        scores = jnp.einsum('tgrd,ngd->grtn', query_heads, key_heads) * scale
        rows = jnp.arange(TOK_DEV, dtype=jnp.int32)
        local_mask = (seg_blk[:, None] == seg_blk[None, :]) & (rows[None, :] <= rows[:, None])
        mask = jnp.concatenate([jnp.ones((TOK_DEV, PREFIX), dtype=bool), local_mask], 1)
        scores = jnp.where(mask[None, None], scores, jnp.float32(-1e+30))
        top = lax.optimization_barrier(jnp.max(scores, axis=-1))
        weights = jnp.exp(scores - top[..., None])
        totals = lax.optimization_barrier(jnp.sum(weights, axis=-1))
        probs = weights.astype(jnp.bfloat16).astype(jnp.float32)
        accum = jnp.einsum('grtn,ngd->grtd', probs, value_heads)
        attended = (accum / totals[..., None]).transpose(2, 0, 1, 3).reshape(TOK_DEV, ATT).astype(jnp.bfloat16)
        hidden = resid_blk.astype(jnp.float32) + jnp.dot(attended, o_weight, preferred_element_type=jnp.float32)
        inv = lax.rsqrt(lax.optimization_barrier(jnp.mean(hidden * hidden, axis=-1, keepdims=True)) + 1e-06)
        normed = (hidden * inv * norm_gain).astype(jnp.bfloat16)
        logits = jnp.dot(normed, router, preferred_element_type=jnp.float32)
        onehot = route_blk[:, :, None] == expert_ids[None, None, :]
        chosen = lax.optimization_barrier(jnp.sum(jnp.where(onehot, logits[:, None, :], 0.0), axis=-1))
        sig = jax.nn.sigmoid(chosen)
        gates = (sig / lax.optimization_barrier(jnp.sum(sig, axis=-1, keepdims=True))).astype(jnp.bfloat16)
        flat = onehot.reshape(TOK_DEV * TOPK, EXPERTS).astype(jnp.int32)
        before = jnp.cumsum(flat, axis=0) - flat
        slot = lax.optimization_barrier(jnp.sum(before * flat, axis=-1)).reshape(TOK_DEV, TOPK)
        place = route_blk * CAP + slot
        hits = place[None, :, :] == slot_ids[:, None, None]
        table = lax.optimization_barrier(jnp.sum(hits.astype(jnp.float32), axis=-1)).astype(jnp.bfloat16)
        dispatch = jnp.dot(table, normed, preferred_element_type=jnp.float32).astype(jnp.bfloat16)
        dispatch = dispatch.reshape(EXPERTS, CAP, D).astype(jnp.float32)
        gate_up = jnp.einsum('ecd,edf->ecf', dispatch, gate_up_full)
        act = (jax.nn.silu(gate_up[..., :FFE]) * gate_up[..., FFE:]).astype(jnp.bfloat16)
        expert_out = jnp.einsum('ecf,efd->ecd', act.astype(jnp.float32), down_full).astype(jnp.bfloat16)
        back_hits = place[:, :, None] == slot_ids[None, None, :]
        ctable = lax.optimization_barrier(jnp.sum(jnp.where(back_hits, gates[:, :, None].astype(jnp.float32), 0.0), axis=1)).astype(jnp.bfloat16)
        mixed = jnp.dot(ctable, expert_out.reshape(EXPERTS * CAP, D), preferred_element_type=jnp.float32)
        return (hidden + mixed).astype(jnp.bfloat16)
    out = lax.map(one_block, jnp.arange(blocks, dtype=jnp.int32))
    return out.reshape(TOKENS, D)
```

```python
import functools

import jax
import jax.numpy as jnp
import numpy as np
from jax import lax
from jax.experimental import pallas as pl
from jax.experimental.pallas import tpu as pltpu
from jax.sharding import PartitionSpec as P

D = 1536
KVH = 8
FFE = 512
CAP = 48
EXPERTS = 32
TOK = 128
ROWS = 144
BF = jnp.bfloat16
F32 = jnp.float32
MESH = pl.DeviceIdType.MESH


def spread_matrix():
    out = np.zeros((384, 512), np.float32)
    for q in range(512):
        i, z, x, c = q % 8, (q // 8) % 8, (q // 64) % 4, q // 256
        if i < 6:
            out[((z % 2) * 32 + x * 8 + (z // 2) * 2 + c) * 6 + i, q] = 1.0
    return out


class Copies:
    def __init__(self, send, recv):
        self.send, self.recv, self.sends, self.recvs, self.open = send, recv, 0, 0, []

    def slot(self):
        self.recvs += 1
        return self.recvs - 1

    def start(self, src, dst, slot, device, again=None):
        copy = pltpu.make_async_remote_copy(
            src_ref=src,
            dst_ref=dst,
            send_sem=self.send.at[self.sends],
            recv_sem=self.recv.at[slot],
            device_id=device,
            device_id_type=MESH,
        )
        self.open.append((self.sends, again or (lambda: src)))
        self.sends += 1
        copy.start()

    def arrived(self, ref, slot):
        pltpu.make_async_copy(ref, ref, self.recv.at[slot]).wait()

    def drain(self):
        for index, source in self.open:
            ref = source()
            pltpu.make_async_copy(ref, ref, self.send.at[index]).wait()


def kernel(
    resid,
    queries,
    suffix,
    kv_own,
    seg_row,
    seg_col,
    o_own,
    spread,
    gain,
    router_t,
    routes_t,
    w1_own,
    w2_own,
    out,
    KV,
    O,
    W1,
    W2,
    XG,
    QH,
    OH,
    AP,
    MK,
    HID,
    XD,
    Y,
    CM,
    PF,
    CS,
    CR,
    S1S,
    S1R,
    S2S,
    S2R,
    ZS,
    ZR,
    send_sem,
    recv_sem,
    local_sem,
):
    grp, dev = lax.axis_index("grp"), lax.axis_index("dev")
    y, zl = lax.div(grp, 2), lax.rem(grp, 2)
    x, zh, c = lax.div(dev, 8), lax.rem(lax.div(dev, 2), 4), lax.rem(dev, 2)

    def at(x_=x, y_=y, zh_=zh, zl_=zl, c_=c):
        return (y_ * 2 + zl_, x_ * 8 + zh_ * 2 + c_)

    def up(v, k=1):
        return lax.rem(v + k, 4)

    right, left, partner = at(x_=up(x)), at(x_=up(x, 3)), at(c_=1 - c)
    sides = (right, left)
    y_sides = (at(y_=up(y)), at(y_=up(y, 3)))
    beside = at(zl_=1 - zl)

    barrier = pltpu.get_barrier_semaphore()
    friends = [right, left, partner, y_sides[0], y_sides[1], at(y_=up(y, 2)), beside]
    for k in (1, 2, 3):
        friends += [at(zh_=up(zh, k)), at(zh_=up(zh, k), zl_=1 - zl)]
    for friend in friends:
        pl.semaphore_signal(barrier, inc=1, device_id=friend, device_id_type=MESH)
    pl.semaphore_wait(barrier, len(friends))

    cp = Copies(send_sem, recv_sem)

    def kv_slot(x_, zh_, c_=c):
        return x_ * 8 + zh_ * 2 + c_

    kv_z = [None] + [cp.slot() for _ in range(3)]
    kv_x = [[cp.slot() for _ in range(2)] for _ in range(4)]
    kv_half = [[cp.slot() for _ in range(2)] for _ in range(4)]
    kv_p = [[cp.slot() for _ in range(4)] for _ in range(4)]
    o_z = [[cp.slot() for _ in range(2)] for _ in range(4)]
    o_y = [None] + [cp.slot() for _ in range(3)]
    o_x = [cp.slot() for _ in range(2)]
    o_half = [cp.slot() for _ in range(2)]
    o_p = [cp.slot() for _ in range(4)]
    w_z = [[[cp.slot() for _ in range(3)] for _ in range(2)] for _ in range(2)]
    w_y = [[[cp.slot() for _ in range(3)] for _ in range(2)] for _ in range(2)]
    w_half = [[[cp.slot() for _ in range(3)] for _ in range(2)] for _ in range(2)]
    t_zl = cp.slot()
    t_x = [[cp.slot() for _ in range(2)] for _ in range(2)]
    t_half = [[cp.slot() for _ in range(2)] for _ in range(2)]
    t_p = [[cp.slot() for _ in range(4)] for _ in range(2)]
    s_c = cp.recvs
    for _ in range(8):
        cp.slot()
    s_1 = [[cp.slot() for _ in range(2)] for _ in range(2)]
    s_2 = [[cp.slot() for _ in range(2)] for _ in range(2)]
    s_z = cp.slot()

    mine = KV.at[kv_slot(x, zh)]
    local_kv = pltpu.make_async_copy(kv_own, mine, local_sem.at[0])
    local_kv.start()
    for k in (1, 2, 3):
        cp.start(kv_own, mine, kv_z[k], at(zh_=up(zh, k)))
    for i in range(2):
        cp.start(kv_own, mine, kv_x[0][i], sides[i])
    cp.start(kv_own, mine, kv_p[0][0], partner)

    my_z = zh * 2 + zl
    o_mine = O.at[y, c, x, my_z]
    local_o = pltpu.make_async_copy(o_own, o_mine, local_sem.at[1])
    local_o.start()
    for k in range(4):
        for j in range(2):
            if k or j:
                cp.start(o_own, o_mine, o_z[k][j], at(zh_=up(zh, k), zl_=zl if j == 0 else 1 - zl))

    pieces = (
        lambda j, y_, z_: W1.at[j, y_, z_, 0],
        lambda j, y_, z_: W1.at[j, y_, z_, 1],
        lambda j, y_, z_: W2.at[j, y_, z_],
    )
    own_pieces = (w1_own.at[0], w1_own.at[1], w2_own)
    w_target = lax.div(zh, 2)
    w_started = []

    def w_start(n):
        for j in range(2):
            for z_ in range(2):

                @pl.when((lax.rem(zh, 2) == j) & (zl == z_))
                def _():
                    for k in range(4):
                        sem = send_sem.at[cp.sends + k]
                        copy = pltpu.make_async_remote_copy(
                            src_ref=own_pieces[n],
                            dst_ref=pieces[n](j, y, z_),
                            send_sem=sem,
                            recv_sem=recv_sem.at[w_z[j][z_][n]],
                            device_id=at(zh_=up(zh, k), zl_=w_target),
                            device_id_type=MESH,
                        )
                        if k:
                            copy.start()
                        else:

                            @pl.when(w_target != zl)
                            def _():
                                copy.start()

                            @pl.when(w_target == zl)
                            def _():
                                pltpu.make_async_copy(
                                    own_pieces[n], pieces[n](j, y, z_), recv_sem.at[w_z[j][z_][n]]
                                ).start()

        w_started.append((n, cp.sends))
        cp.sends += 4

    def w_drain():
        for n, first in w_started:
            for k in range(4):
                copy = pltpu.make_async_remote_copy(
                    src_ref=own_pieces[n],
                    dst_ref=pieces[n](0, y, 0),
                    send_sem=send_sem.at[first + k],
                    recv_sem=recv_sem.at[w_z[0][0][n]],
                    device_id=at(zh_=up(zh, k), zl_=w_target),
                    device_id_type=MESH,
                )
                if k:
                    copy.wait_send()
                else:

                    @pl.when(w_target != zl)
                    def _():
                        copy.wait_send()

    def w_along_y(n):
        for j in range(2):
            for z_ in range(2):
                cp.arrived(pieces[n](j, y, z_), w_z[j][z_][n])
            both = pieces[n](j, y, slice(None))
            for i in range(2):
                cp.start(both, both, w_y[j][i][n], y_sides[i])

    def w_forward(n):
        for j in range(2):
            for i in range(2):
                origin = up(y, 3) if i == 0 else up(y)
                cp.arrived(pieces[n](j, origin, slice(None)), w_y[j][i][n])
                half = pieces[n](j, origin, i)
                cp.start(half, half, w_half[j][i][n], y_sides[i])

    def w_finish(n):
        for j in range(2):
            for i in range(2):
                cp.arrived(pieces[n](j, up(y, 2), i), w_half[j][i][n])

    for n in range(3):
        w_start(n)

    lane = lax.broadcasted_iota(jnp.int32, (TOK, 128), 1)
    low = lane < 64
    for p in range(4):
        tiles = [queries[:, p * 384 + 128 * i : p * 384 + 128 * (i + 1)].astype(F32) * 0.125 for i in range(3)]
        turned = [pltpu.roll(t, 64, 1) for t in (tiles[0], tiles[2])]
        heads = (
            jnp.where(low, tiles[0], 0.0),
            jnp.where(low, turned[0], 0.0),
            jnp.where(low, tiles[1], 0.0),
            jnp.where(low, 0.0, tiles[1]),
            jnp.where(low, 0.0, turned[1]),
            jnp.where(low, 0.0, tiles[2]),
        )
        for h in range(6):
            QH[2 * p + h // 3, (h % 3) * 128 : (h % 3 + 1) * 128, :] = heads[h].astype(BF)
    row = lax.broadcasted_iota(jnp.int32, (TOK, TOK), 0)
    col = lax.broadcasted_iota(jnp.int32, (TOK, TOK), 1)
    allowed = (seg_row[...] == seg_col[...]) & (col <= row)
    bias = jnp.where(allowed, 0.0, -1e30)
    for i in range(3):
        MK[i * 128 : (i + 1) * 128, :] = bias

    for k in (1, 2, 3):
        piece = KV.at[kv_slot(x, up(zh, 4 - k))]
        cp.arrived(piece, kv_z[k])
        for i in range(2):
            cp.start(piece, piece, kv_x[k][i], sides[i])
        cp.start(piece, piece, kv_p[k][0], partner)
    for k in range(4):
        for i in range(2):
            slot = kv_slot(up(x, 3) if i == 0 else up(x), up(zh, 4 - k))
            piece = KV.at[slot]
            cp.arrived(piece, kv_x[k][i])
            half = KV.at[slot, 32 * i : 32 * (i + 1)]
            cp.start(half, half, kv_half[k][i], sides[i])
            cp.start(piece, piece, kv_p[k][1 + i], partner)
    local_o.wait()
    for k in range(4):
        for j in range(2):
            if k or j:
                zz = up(zh, 4 - k) * 2 + (zl if j == 0 else 1 - zl)
                cp.arrived(O.at[y, c, x, zz], o_z[k][j])
    for k in (1, 2, 3):
        cp.start(O.at[y, c, x], O.at[y, c, x], o_y[k], at(y_=up(y, k)))
    for k in range(4):
        slot = kv_slot(up(x, 2), up(zh, 4 - k))
        for i in range(2):
            cp.arrived(KV.at[slot, 32 * i : 32 * (i + 1)], kv_half[k][i])
        cp.start(KV.at[slot], KV.at[slot], kv_p[k][3], partner)
    for k in (1, 2, 3):
        cp.arrived(O.at[up(y, 4 - k), c, x], o_y[k])
    for i in range(2):
        cp.start(O.at[:, c, x], O.at[:, c, x], o_x[i], sides[i])
    cp.start(O.at[:, c, x], O.at[:, c, x], o_p[0], partner)
    for k in range(4):
        for i, from_x in enumerate((x, up(x, 3), up(x), up(x, 2))):
            cp.arrived(KV.at[kv_slot(from_x, up(zh, 4 - k), 1 - c)], kv_p[k][i])
    local_kv.wait()

    nt = (((1,), (1,)), ((), ()))

    def attend(h):
        p = lax.div(h, 2)
        k_cols = pl.ds(pl.multiple_of(p * 128, 128), 128)
        v_cols = pl.ds(pl.multiple_of(512 + p * 128, 128), 128)
        q = QH[h]
        s1 = lax.dot_general(q, KV[:, :, k_cols].reshape(2048, 128), nt, preferred_element_type=F32)
        s2 = lax.dot_general(q, suffix[:, k_cols], nt, preferred_element_type=F32) + MK[...]
        top = jnp.maximum(jnp.max(s1, axis=1, keepdims=True), jnp.max(s2, axis=1, keepdims=True))
        p1, p2 = jnp.exp(s1 - top), jnp.exp(s2 - top)
        total = jnp.sum(p1, axis=1, keepdims=True) + jnp.sum(p2, axis=1, keepdims=True)
        acc = jnp.dot(p1.astype(BF), KV[:, :, v_cols].reshape(2048, 128), preferred_element_type=F32)
        acc += jnp.dot(p2.astype(BF), suffix[:, v_cols], preferred_element_type=F32)
        OH[h] = acc / total

    @pl.loop(0, 2)
    def _(h):
        attend(h)

    w_along_y(0)

    @pl.loop(2, 5)
    def _(h):
        attend(h)

    w_along_y(1)
    for i in range(2):
        origin = up(x, 3) if i == 0 else up(x)
        cp.arrived(O.at[:, c, origin], o_x[i])
        half = O.at[pl.ds(2 * i, 2), c, origin]
        cp.start(half, half, o_half[i], sides[i])
        cp.start(O.at[:, c, origin], O.at[:, c, origin], o_p[1 + i], partner)

    @pl.loop(5, 8)
    def _(h):
        attend(h)

    for p in range(4):
        a = [OH[2 * p + h // 3, (h % 3) * 128 : (h % 3 + 1) * 128, :] for h in range(6)]
        tiles = (
            jnp.where(low, a[0], pltpu.roll(a[1], 64, 1)),
            jnp.where(low, a[2], a[3]),
            jnp.where(low, pltpu.roll(a[4], 64, 1), a[5]),
        )
        att = jnp.concatenate([t.astype(BF) for t in tiles], axis=1)
        AP[p] = jnp.dot(att, spread[...], preferred_element_type=F32).astype(BF)

    far = up(x, 2)
    for i in range(2):
        cp.arrived(O.at[pl.ds(2 * i, 2), c, far], o_half[i])
    cp.start(O.at[:, c, far], O.at[:, c, far], o_p[3], partner)
    w_along_y(2)
    for i, from_x in enumerate((x, up(x, 3), up(x), far)):
        cp.arrived(O.at[:, 1 - c, from_x], o_p[i])

    total = resid[...].astype(F32)
    for p in range(4):
        total += jnp.dot(AP[p], O[p].reshape(512, D), preferred_element_type=F32)
    HID[...] = total
    scale = lax.rsqrt(jnp.mean(total * total, axis=1, keepdims=True) + 1e-06)
    normed = (total * scale * gain[...]).astype(BF)
    logits = lax.dot_general(router_t[...], normed, nt, preferred_element_type=F32)
    expert = lax.broadcasted_iota(jnp.int32, (EXPERTS, TOK), 0)
    chosen = routes_t[0:1, :] == expert
    for k in range(1, 8):
        chosen = chosen | (routes_t[k : k + 1, :] == expert)
    sig = jnp.where(chosen, 1.0 / (1.0 + jnp.exp(-logits)), 0.0)
    gates = sig / jnp.sum(sig, axis=0, keepdims=True)
    upper = jnp.where(row <= col, 1.0, 0.0).astype(BF)
    hit = jnp.where(chosen, 1.0, 0.0)
    rank = jnp.dot(hit.astype(BF), upper, preferred_element_type=F32)
    rank = jnp.where(chosen, rank - 1.0, -1.0)

    def tok(x_, z_, c_=c):
        return (c_ * 4 + x_) * 2 + z_

    own = tok(x, zl)
    XG[own, 0:TOK, :] = normed
    for n in range(4):
        XG[own, TOK : TOK + 16, 128 * n : 128 * (n + 1)] = jnp.concatenate(
            [gates[8 * n : 8 * n + 8], rank[8 * n : 8 * n + 8]], axis=0
        ).astype(BF)
    cp.start(XG.at[own], XG.at[own], t_zl, beside)
    for i in range(2):
        cp.start(XG.at[own], XG.at[own], t_x[0][i], sides[i])
    cp.start(XG.at[own], XG.at[own], t_p[0][0], partner)
    piece = XG.at[tok(x, 1 - zl)]
    cp.arrived(piece, t_zl)
    for i in range(2):
        cp.start(piece, piece, t_x[1][i], sides[i])
    cp.start(piece, piece, t_p[1][0], partner)
    w_forward(0)
    cuts = ((0, 64), (64, ROWS - 64))
    for r in range(2):
        z_ = zl if r == 0 else 1 - zl
        for i in range(2):
            slot = tok(up(x, 3) if i == 0 else up(x), z_)
            cp.arrived(XG.at[slot], t_x[r][i])
            half = XG.at[slot, pl.ds(*cuts[i])]
            cp.start(half, half, t_half[r][i], sides[i])
            cp.start(XG.at[slot], XG.at[slot], t_p[r][1 + i], partner)
    w_forward(1)
    for r in range(2):
        z_ = zl if r == 0 else 1 - zl
        slot = tok(far, z_)
        for i in range(2):
            cp.arrived(XG.at[slot, pl.ds(*cuts[i])], t_half[r][i])
        cp.start(XG.at[slot], XG.at[slot], t_p[r][3], partner)
    w_forward(2)
    for r in range(2):
        z_ = zl if r == 0 else 1 - zl
        for i, from_x in enumerate((x, up(x, 3), up(x), far)):
            cp.arrived(XG.at[tok(from_x, z_, 1 - c)], t_p[r][i])
    for n in range(3):
        w_finish(n)

    e_cols = pl.ds(pl.multiple_of(x * 128, 128), 128)
    slot_row = lax.broadcasted_iota(jnp.int32, (TOK, TOK), 0)
    slot_f = jnp.where(slot_row < CAP, slot_row, slot_row - CAP).astype(F32)
    first = slot_row < CAP
    sub = lax.broadcasted_iota(jnp.int32, (8, TOK), 0)
    picks = [sub == (2 * zl + j) * 2 + c for j in range(2)]
    sources = [(rel_c, rel_z) for rel_c in range(2) for rel_z in range(2)]
    Y[...] = jnp.zeros_like(Y)

    first_c = cp.sends
    cp.sends += 8

    def chunk_copy(n):
        return pltpu.make_async_remote_copy(
            src_ref=CS.at[n],
            dst_ref=CR.at[n],
            send_sem=send_sem.at[first_c + n],
            recv_sem=recv_sem.at[s_c + n],
            device_id=partner,
            device_id_type=MESH,
        )

    def chunk(n):
        from_x = lax.rem(x + 2 - n + 3 * lax.div(n, 2) - 2 * lax.div(n, 3), 4)
        for s, (rel_c, rel_z) in enumerate(sources):
            slot = tok(from_x, lax.rem(zl + rel_z, 2), lax.rem(c + rel_c, 2))
            info = XG[slot, TOK : TOK + 16, e_cols].astype(F32)
            gate, rank = [
                [jnp.sum(jnp.where(pick, part, 0.0), axis=0, keepdims=True) for pick in picks]
                for part in (info[0:8], info[8:16])
            ]
            here = jnp.where(first, rank[0], rank[1]) == slot_f
            table = jnp.where(here, 1.0, 0.0).astype(BF)
            CM[s] = jnp.where(here, jnp.where(first, gate[0], gate[1]), 0.0).T.astype(BF)
            rows = jnp.dot(table, XG[slot, 0:TOK, :], preferred_element_type=F32).astype(BF)
            XD[0, s * CAP : (s + 1) * CAP, :] = rows[0:CAP]
            XD[1, s * CAP : (s + 1) * CAP, :] = rows[CAP : 2 * CAP]
        for j in range(2):
            gu = jnp.dot(XD[j], W1[j].reshape(D, 2 * FFE), preferred_element_type=F32)
            g, u = gu[:, :FFE], gu[:, FFE:]
            act = (g / (1.0 + jnp.exp(-g)) * u).astype(BF)
            res = jnp.dot(act, W2[j].reshape(FFE, D), preferred_element_type=F32).astype(BF)
            for s in range(4):
                Y[s, j * CAP : (j + 1) * CAP, :] = res[s * CAP : (s + 1) * CAP]
        for s, (rel_c, rel_z) in enumerate(sources):
            part = jnp.dot(CM[s], Y[s], preferred_element_type=F32)
            if rel_c == 0:
                PF[n * 2 + rel_z] = part
            else:
                CS[n * 2 + rel_z] = part.astype(BF)
                chunk_copy(n * 2 + rel_z).start()

    def summed(n, r):
        cp.arrived(CR.at[2 * n + r], s_c + 2 * n + r)
        return PF[2 * n + r] + CR[2 * n + r].astype(F32)

    def reduce_far():
        for r in range(2):
            S1S[r] = summed(0, r).astype(BF)
            for i in range(2):
                cut = pl.ds(64 * i, 64)
                cp.start(
                    S1S.at[r, cut],
                    S1R.at[r, cut],
                    s_1[r][i],
                    sides[i],
                    functools.partial(lambda r, i: S1S.at[r, pl.ds(64 * i, 64)], r, i),
                )

    def reduce_side(i):
        for r in range(2):
            part = summed(1 + i, r)
            cut = pl.ds(64 * i, 64)
            cp.arrived(S1R.at[r, cut], s_1[r][i])
            S2S[i, r] = part.astype(BF)
            S2S[i, r, cut, :] = (part[64 * i : 64 * i + 64] + S1R[r, cut, :].astype(F32)).astype(BF)
            cp.start(
                S2S.at[i, r],
                S2R.at[i, r],
                s_2[i][r],
                sides[i],
                functools.partial(lambda i, r: S2S.at[i, r], i, r),
            )

    @pl.loop(0, 4)
    def _(n):
        chunk(n)

        @pl.when(n == 1)
        def _():
            reduce_far()

        @pl.when(n == 2)
        def _():
            reduce_side(0)

        @pl.when(n == 3)
        def _():
            reduce_side(1)

    for r in (1, 0):
        part = summed(3, r)
        for i in range(2):
            cp.arrived(S2R.at[i, r], s_2[i][r])
            part += S2R[i, r].astype(F32)
        if r == 1:
            ZS[...] = part.astype(BF)
            cp.start(ZS, ZR, s_z, beside)
    cp.arrived(ZR, s_z)
    out[...] = (HID[...] + part + ZR[...].astype(F32)).astype(BF)

    for n in range(8):
        chunk_copy(n).wait_send()
    w_drain()
    cp.drain()


def per_device(
    resid, queries, suffix_kv, prefix_kv, segments, o_weight, norm_gain, router, routes, w_gate_up, w_down
):
    vm = pl.BlockSpec(memory_space=pltpu.VMEM)
    hbm = pl.BlockSpec(memory_space=pl.ANY)
    args = (
        resid,
        queries,
        suffix_kv.reshape(TOK, 1024),
        prefix_kv.reshape(64, 1024),
        segments,
        segments.reshape(TOK, 1),
        jnp.pad(o_weight, ((0, 2), (0, 0))),
        jnp.asarray(spread_matrix(), BF),
        norm_gain.reshape(1, D),
        router.T,
        routes.T,
        w_gate_up.reshape(2, 96, 1024),
        w_down.reshape(64, D),
    )
    specs = [vm, vm, vm, hbm, vm, vm, hbm, vm, vm, vm, vm, hbm, hbm]
    return pl.pallas_call(
        kernel,
        out_shape=jax.ShapeDtypeStruct((TOK, D), BF),
        in_specs=specs,
        out_specs=vm,
        scratch_shapes=[
            pltpu.VMEM((32, 64, 1024), BF),
            pltpu.VMEM((4, 2, 4, 8, 8, D), BF),
            pltpu.VMEM((2, 4, 2, 2, 96, 1024), BF),
            pltpu.VMEM((2, 4, 2, 64, D), BF),
            pltpu.VMEM((16, ROWS, D), BF),
            pltpu.VMEM((8, 384, 128), BF),
            pltpu.VMEM((8, 384, 128), F32),
            pltpu.VMEM((4, TOK, 512), BF),
            pltpu.VMEM((384, TOK), F32),
            pltpu.VMEM((TOK, D), F32),
            pltpu.VMEM((2, 4 * CAP, D), BF),
            pltpu.VMEM((4, TOK, D), BF),
            pltpu.VMEM((4, TOK, TOK), BF),
            pltpu.VMEM((8, TOK, D), F32),
            pltpu.VMEM((8, TOK, D), BF),
            pltpu.VMEM((8, TOK, D), BF),
            pltpu.VMEM((2, TOK, D), BF),
            pltpu.VMEM((2, TOK, D), BF),
            pltpu.VMEM((2, 2, TOK, D), BF),
            pltpu.VMEM((2, 2, TOK, D), BF),
            pltpu.VMEM((TOK, D), BF),
            pltpu.VMEM((TOK, D), BF),
            pltpu.SemaphoreType.DMA((192,)),
            pltpu.SemaphoreType.DMA((192,)),
            pltpu.SemaphoreType.DMA((2,)),
        ],
        compiler_params=pltpu.CompilerParams(
            collective_id=0, has_side_effects=True, vmem_limit_bytes=67043328
        ),
    )(*args)


def solution(mesh):
    return jax.shard_map(
        per_device,
        mesh=mesh,
        in_specs=(
            P(("grp", "dev"), None),
            P(("grp", "dev"), None),
            P(("grp", "dev"), None, None),
            P("grp", "dev", None, None),
            P(("grp", "dev"), None),
            P(("grp", "dev"), None),
            P(),
            P(),
            P(("grp", "dev"), None),
            P("dev", "grp", None),
            P("dev", "grp", None),
        ),
        out_specs=P(("grp", "dev"), None),
        check_vma=False,
    )
```

```python
import functools

import jax
import jax.numpy as jnp
import numpy as np
from jax import lax
from jax.experimental import pallas as pl
from jax.experimental.pallas import tpu as pltpu
from jax.sharding import PartitionSpec as P

D = 1536
KVH = 8
FFE = 512
CAP = 48
EXPERTS = 32
TOK = 128
ROWS = 144
BF = jnp.bfloat16
F32 = jnp.float32
MESH = pl.DeviceIdType.MESH


def spread_matrix():
    out = np.zeros((384, 512), np.float32)
    for q in range(512):
        i, z, x, c = q % 8, (q // 8) % 8, (q // 64) % 4, q // 256
        if i < 6:
            out[((z % 2) * 32 + x * 8 + (z // 2) * 2 + c) * 6 + i, q] = 1.0
    return out


class Copies:
    def __init__(self, send, recv):
        self.send, self.recv, self.sends, self.recvs, self.open = send, recv, 0, 0, []

    def slot(self):
        self.recvs += 1
        return self.recvs - 1

    def start(self, src, dst, slot, device, again=None):
        copy = pltpu.make_async_remote_copy(
            src_ref=src,
            dst_ref=dst,
            send_sem=self.send.at[self.sends],
            recv_sem=self.recv.at[slot],
            device_id=device,
            device_id_type=MESH,
        )
        self.open.append((self.sends, again or (lambda: src)))
        self.sends += 1
        copy.start()

    def arrived(self, ref, slot):
        pltpu.make_async_copy(ref, ref, self.recv.at[slot]).wait()

    def drain(self):
        for index, source in self.open:
            ref = source()
            pltpu.make_async_copy(ref, ref, self.send.at[index]).wait()


def kernel(
    resid,
    queries,
    suffix,
    kv_own,
    seg_row,
    seg_col,
    o_own,
    spread,
    gain,
    router_t,
    routes_t,
    w1_own,
    w2_own,
    out,
    KV,
    O,
    W1,
    W2,
    XG,
    QH,
    OH,
    AP,
    MK,
    HID,
    XD,
    Y,
    CM,
    PF,
    CS,
    CR,
    S1S,
    S1R,
    S2S,
    S2R,
    ZS,
    ZR,
    send_sem,
    recv_sem,
    local_sem,
):
    grp, dev = lax.axis_index("grp"), lax.axis_index("dev")
    y, zl = lax.div(grp, 2), lax.rem(grp, 2)
    x, zh, c = lax.div(dev, 8), lax.rem(lax.div(dev, 2), 4), lax.rem(dev, 2)

    def at(x_=x, y_=y, zh_=zh, zl_=zl, c_=c):
        return (y_ * 2 + zl_, x_ * 8 + zh_ * 2 + c_)

    def up(v, k=1):
        return lax.rem(v + k, 4)

    right, left, partner = at(x_=up(x)), at(x_=up(x, 3)), at(c_=1 - c)
    sides = (right, left)
    y_sides = (at(y_=up(y)), at(y_=up(y, 3)))
    beside = at(zl_=1 - zl)

    barrier = pltpu.get_barrier_semaphore()
    friends = [right, left, partner, y_sides[0], y_sides[1], at(y_=up(y, 2)), beside]
    for k in (1, 2, 3):
        friends += [at(zh_=up(zh, k)), at(zh_=up(zh, k), zl_=1 - zl)]
    for friend in friends:
        pl.semaphore_signal(barrier, inc=1, device_id=friend, device_id_type=MESH)
    pl.semaphore_wait(barrier, len(friends))

    cp = Copies(send_sem, recv_sem)

    def kv_slot(x_, zh_, c_=c):
        return x_ * 8 + zh_ * 2 + c_

    kv_z = [None] + [cp.slot() for _ in range(3)]
    kv_x = [[cp.slot() for _ in range(2)] for _ in range(4)]
    kv_half = [[cp.slot() for _ in range(2)] for _ in range(4)]
    kv_p = [[cp.slot() for _ in range(4)] for _ in range(4)]
    o_z = [[cp.slot() for _ in range(2)] for _ in range(4)]
    o_y = [None] + [cp.slot() for _ in range(3)]
    o_x = [cp.slot() for _ in range(2)]
    o_half = [cp.slot() for _ in range(2)]
    o_p = [cp.slot() for _ in range(4)]
    w_z = [[[cp.slot() for _ in range(3)] for _ in range(2)] for _ in range(2)]
    w_y = [[[cp.slot() for _ in range(3)] for _ in range(2)] for _ in range(2)]
    w_half = [[[cp.slot() for _ in range(3)] for _ in range(2)] for _ in range(2)]
    t_zl = cp.slot()
    t_x = [[cp.slot() for _ in range(2)] for _ in range(2)]
    t_half = [[cp.slot() for _ in range(2)] for _ in range(2)]
    t_p = [[cp.slot() for _ in range(4)] for _ in range(2)]
    s_c = cp.recvs
    for _ in range(8):
        cp.slot()
    s_1 = [[cp.slot() for _ in range(2)] for _ in range(2)]
    s_2 = [[cp.slot() for _ in range(2)] for _ in range(2)]
    s_z = cp.slot()

    mine = KV.at[kv_slot(x, zh)]
    local_kv = pltpu.make_async_copy(kv_own, mine, local_sem.at[0])
    local_kv.start()
    for k in (1, 2, 3):
        cp.start(kv_own, mine, kv_z[k], at(zh_=up(zh, k)))
    for i in range(2):
        cp.start(kv_own, mine, kv_x[0][i], sides[i])
    cp.start(kv_own, mine, kv_p[0][0], partner)

    my_z = zh * 2 + zl
    o_mine = O.at[y, c, x, my_z]
    local_o = pltpu.make_async_copy(o_own, o_mine, local_sem.at[1])
    local_o.start()
    for k in range(4):
        for j in range(2):
            if k or j:
                cp.start(o_own, o_mine, o_z[k][j], at(zh_=up(zh, k), zl_=zl if j == 0 else 1 - zl))

    pieces = (
        lambda j, y_, z_: W1.at[j, y_, z_, 0],
        lambda j, y_, z_: W1.at[j, y_, z_, 1],
        lambda j, y_, z_: W2.at[j, y_, z_],
    )
    own_pieces = (w1_own.at[0], w1_own.at[1], w2_own)
    w_target = lax.div(zh, 2)
    w_started = []

    def w_start(n):
        for j in range(2):
            for z_ in range(2):

                @pl.when((lax.rem(zh, 2) == j) & (zl == z_))
                def _():
                    for k in range(4):
                        sem = send_sem.at[cp.sends + k]
                        copy = pltpu.make_async_remote_copy(
                            src_ref=own_pieces[n],
                            dst_ref=pieces[n](j, y, z_),
                            send_sem=sem,
                            recv_sem=recv_sem.at[w_z[j][z_][n]],
                            device_id=at(zh_=up(zh, k), zl_=w_target),
                            device_id_type=MESH,
                        )
                        if k:
                            copy.start()
                        else:

                            @pl.when(w_target != zl)
                            def _():
                                copy.start()

                            @pl.when(w_target == zl)
                            def _():
                                pltpu.make_async_copy(
                                    own_pieces[n], pieces[n](j, y, z_), recv_sem.at[w_z[j][z_][n]]
                                ).start()

        w_started.append((n, cp.sends))
        cp.sends += 4

    def w_drain():
        for n, first in w_started:
            for k in range(4):
                copy = pltpu.make_async_remote_copy(
                    src_ref=own_pieces[n],
                    dst_ref=pieces[n](0, y, 0),
                    send_sem=send_sem.at[first + k],
                    recv_sem=recv_sem.at[w_z[0][0][n]],
                    device_id=at(zh_=up(zh, k), zl_=w_target),
                    device_id_type=MESH,
                )
                if k:
                    copy.wait_send()
                else:

                    @pl.when(w_target != zl)
                    def _():
                        copy.wait_send()

    def w_along_y(n):
        for j in range(2):
            for z_ in range(2):
                cp.arrived(pieces[n](j, y, z_), w_z[j][z_][n])
            both = pieces[n](j, y, slice(None))
            for i in range(2):
                cp.start(both, both, w_y[j][i][n], y_sides[i])

    def w_forward(n):
        for j in range(2):
            for i in range(2):
                origin = up(y, 3) if i == 0 else up(y)
                cp.arrived(pieces[n](j, origin, slice(None)), w_y[j][i][n])
                half = pieces[n](j, origin, i)
                cp.start(half, half, w_half[j][i][n], y_sides[i])

    def w_finish(n):
        for j in range(2):
            for i in range(2):
                cp.arrived(pieces[n](j, up(y, 2), i), w_half[j][i][n])

    for n in range(3):
        w_start(n)

    lane = lax.broadcasted_iota(jnp.int32, (TOK, 128), 1)
    low = lane < 64
    for p in range(4):
        tiles = [queries[:, p * 384 + 128 * i : p * 384 + 128 * (i + 1)].astype(F32) * 0.125 for i in range(3)]
        turned = [pltpu.roll(t, 64, 1) for t in (tiles[0], tiles[2])]
        heads = (
            jnp.where(low, tiles[0], 0.0),
            jnp.where(low, turned[0], 0.0),
            jnp.where(low, tiles[1], 0.0),
            jnp.where(low, 0.0, tiles[1]),
            jnp.where(low, 0.0, turned[1]),
            jnp.where(low, 0.0, tiles[2]),
        )
        for h in range(6):
            QH[2 * p + h // 3, (h % 3) * 128 : (h % 3 + 1) * 128, :] = heads[h].astype(BF)
    row = lax.broadcasted_iota(jnp.int32, (TOK, TOK), 0)
    col = lax.broadcasted_iota(jnp.int32, (TOK, TOK), 1)
    allowed = (seg_row[...] == seg_col[...]) & (col <= row)
    bias = jnp.where(allowed, 0.0, -1e30)
    for i in range(3):
        MK[i * 128 : (i + 1) * 128, :] = bias

    for k in (1, 2, 3):
        piece = KV.at[kv_slot(x, up(zh, 4 - k))]
        cp.arrived(piece, kv_z[k])
        for i in range(2):
            cp.start(piece, piece, kv_x[k][i], sides[i])
        cp.start(piece, piece, kv_p[k][0], partner)
    for k in range(4):
        for i in range(2):
            slot = kv_slot(up(x, 3) if i == 0 else up(x), up(zh, 4 - k))
            piece = KV.at[slot]
            cp.arrived(piece, kv_x[k][i])
            half = KV.at[slot, 32 * i : 32 * (i + 1)]
            cp.start(half, half, kv_half[k][i], sides[i])
            cp.start(piece, piece, kv_p[k][1 + i], partner)
    local_o.wait()
    for k in range(4):
        for j in range(2):
            if k or j:
                zz = up(zh, 4 - k) * 2 + (zl if j == 0 else 1 - zl)
                cp.arrived(O.at[y, c, x, zz], o_z[k][j])
    for k in (1, 2, 3):
        cp.start(O.at[y, c, x], O.at[y, c, x], o_y[k], at(y_=up(y, k)))
    w_along_y(0)
    for k in range(4):
        slot = kv_slot(up(x, 2), up(zh, 4 - k))
        for i in range(2):
            cp.arrived(KV.at[slot, 32 * i : 32 * (i + 1)], kv_half[k][i])
        cp.start(KV.at[slot], KV.at[slot], kv_p[k][3], partner)
    for k in (1, 2, 3):
        cp.arrived(O.at[up(y, 4 - k), c, x], o_y[k])
    for i in range(2):
        cp.start(O.at[:, c, x], O.at[:, c, x], o_x[i], sides[i])
    cp.start(O.at[:, c, x], O.at[:, c, x], o_p[0], partner)
    w_along_y(1)
    for k in range(4):
        for i, from_x in enumerate((x, up(x, 3), up(x), up(x, 2))):
            cp.arrived(KV.at[kv_slot(from_x, up(zh, 4 - k), 1 - c)], kv_p[k][i])
    local_kv.wait()

    nt = (((1,), (1,)), ((), ()))

    def attend(h):
        p = lax.div(h, 2)
        k_cols = pl.ds(pl.multiple_of(p * 128, 128), 128)
        v_cols = pl.ds(pl.multiple_of(512 + p * 128, 128), 128)
        q = QH[h]
        s1 = lax.dot_general(q, KV[:, :, k_cols].reshape(2048, 128), nt, preferred_element_type=F32)
        s2 = lax.dot_general(q, suffix[:, k_cols], nt, preferred_element_type=F32) + MK[...]
        top = jnp.maximum(jnp.max(s1, axis=1, keepdims=True), jnp.max(s2, axis=1, keepdims=True))
        p1, p2 = jnp.exp(s1 - top), jnp.exp(s2 - top)
        total = jnp.sum(p1, axis=1, keepdims=True) + jnp.sum(p2, axis=1, keepdims=True)
        acc = jnp.dot(p1.astype(BF), KV[:, :, v_cols].reshape(2048, 128), preferred_element_type=F32)
        acc += jnp.dot(p2.astype(BF), suffix[:, v_cols], preferred_element_type=F32)
        OH[h] = acc / total

    @pl.loop(0, 4)
    def _(h):
        attend(h)

    for i in range(2):
        origin = up(x, 3) if i == 0 else up(x)
        cp.arrived(O.at[:, c, origin], o_x[i])
        half = O.at[pl.ds(2 * i, 2), c, origin]
        cp.start(half, half, o_half[i], sides[i])
        cp.start(O.at[:, c, origin], O.at[:, c, origin], o_p[1 + i], partner)

    w_along_y(2)

    @pl.loop(4, 8)
    def _(h):
        attend(h)

    w_forward(0)

    for p in range(4):
        a = [OH[2 * p + h // 3, (h % 3) * 128 : (h % 3 + 1) * 128, :] for h in range(6)]
        tiles = (
            jnp.where(low, a[0], pltpu.roll(a[1], 64, 1)),
            jnp.where(low, a[2], a[3]),
            jnp.where(low, pltpu.roll(a[4], 64, 1), a[5]),
        )
        att = jnp.concatenate([t.astype(BF) for t in tiles], axis=1)
        AP[p] = jnp.dot(att, spread[...], preferred_element_type=F32).astype(BF)

    far = up(x, 2)
    for i in range(2):
        cp.arrived(O.at[pl.ds(2 * i, 2), c, far], o_half[i])
    cp.start(O.at[:, c, far], O.at[:, c, far], o_p[3], partner)
    for i, from_x in enumerate((x, up(x, 3), up(x), far)):
        cp.arrived(O.at[:, 1 - c, from_x], o_p[i])

    total = resid[...].astype(F32)
    for p in range(4):
        total += jnp.dot(AP[p], O[p].reshape(512, D), preferred_element_type=F32)
    HID[...] = total
    scale = lax.rsqrt(jnp.mean(total * total, axis=1, keepdims=True) + 1e-06)
    normed = (total * scale * gain[...]).astype(BF)
    logits = lax.dot_general(router_t[...], normed, nt, preferred_element_type=F32)
    expert = lax.broadcasted_iota(jnp.int32, (EXPERTS, TOK), 0)
    chosen = routes_t[0:1, :] == expert
    for k in range(1, 8):
        chosen = chosen | (routes_t[k : k + 1, :] == expert)
    sig = jnp.where(chosen, 1.0 / (1.0 + jnp.exp(-logits)), 0.0)
    gates = sig / jnp.sum(sig, axis=0, keepdims=True)
    upper = jnp.where(row <= col, 1.0, 0.0).astype(BF)
    hit = jnp.where(chosen, 1.0, 0.0)
    rank = jnp.dot(hit.astype(BF), upper, preferred_element_type=F32)
    rank = jnp.where(chosen, rank - 1.0, -1.0)

    def tok(x_, z_, c_=c):
        return (c_ * 4 + x_) * 2 + z_

    own = tok(x, zl)
    XG[own, 0:TOK, :] = normed
    for n in range(4):
        XG[own, TOK : TOK + 16, 128 * n : 128 * (n + 1)] = jnp.concatenate(
            [gates[8 * n : 8 * n + 8], rank[8 * n : 8 * n + 8]], axis=0
        ).astype(BF)
    cp.start(XG.at[own], XG.at[own], t_zl, beside)
    for i in range(2):
        cp.start(XG.at[own], XG.at[own], t_x[0][i], sides[i])
    cp.start(XG.at[own], XG.at[own], t_p[0][0], partner)
    piece = XG.at[tok(x, 1 - zl)]
    cp.arrived(piece, t_zl)
    for i in range(2):
        cp.start(piece, piece, t_x[1][i], sides[i])
    cp.start(piece, piece, t_p[1][0], partner)
    w_forward(1)
    cuts = ((0, 64), (64, ROWS - 64))
    for r in range(2):
        z_ = zl if r == 0 else 1 - zl
        for i in range(2):
            slot = tok(up(x, 3) if i == 0 else up(x), z_)
            cp.arrived(XG.at[slot], t_x[r][i])
            half = XG.at[slot, pl.ds(*cuts[i])]
            cp.start(half, half, t_half[r][i], sides[i])
            cp.start(XG.at[slot], XG.at[slot], t_p[r][1 + i], partner)
    w_forward(2)
    for r in range(2):
        z_ = zl if r == 0 else 1 - zl
        slot = tok(far, z_)
        for i in range(2):
            cp.arrived(XG.at[slot, pl.ds(*cuts[i])], t_half[r][i])
        cp.start(XG.at[slot], XG.at[slot], t_p[r][3], partner)
    for r in range(2):
        z_ = zl if r == 0 else 1 - zl
        for i, from_x in enumerate((x, up(x, 3), up(x), far)):
            cp.arrived(XG.at[tok(from_x, z_, 1 - c)], t_p[r][i])
    for n in range(3):
        w_finish(n)

    e_cols = pl.ds(pl.multiple_of(x * 128, 128), 128)
    slot_row = lax.broadcasted_iota(jnp.int32, (TOK, TOK), 0)
    slot_f = jnp.where(slot_row < CAP, slot_row, slot_row - CAP).astype(F32)
    first = slot_row < CAP
    sub = lax.broadcasted_iota(jnp.int32, (8, TOK), 0)
    picks = [sub == (2 * zl + j) * 2 + c for j in range(2)]
    sources = [(rel_c, rel_z) for rel_c in range(2) for rel_z in range(2)]
    Y[...] = jnp.zeros_like(Y)

    first_c = cp.sends
    cp.sends += 8

    def chunk_copy(n):
        return pltpu.make_async_remote_copy(
            src_ref=CS.at[n],
            dst_ref=CR.at[n],
            send_sem=send_sem.at[first_c + n],
            recv_sem=recv_sem.at[s_c + n],
            device_id=partner,
            device_id_type=MESH,
        )

    def chunk(n):
        from_x = lax.rem(x + 2 - n + 3 * lax.div(n, 2) - 2 * lax.div(n, 3), 4)
        for s, (rel_c, rel_z) in enumerate(sources):
            slot = tok(from_x, lax.rem(zl + rel_z, 2), lax.rem(c + rel_c, 2))
            info = XG[slot, TOK : TOK + 16, e_cols].astype(F32)
            gate, rank = [
                [jnp.sum(jnp.where(pick, part, 0.0), axis=0, keepdims=True) for pick in picks]
                for part in (info[0:8], info[8:16])
            ]
            here = jnp.where(first, rank[0], rank[1]) == slot_f
            table = jnp.where(here, 1.0, 0.0).astype(BF)
            CM[s] = jnp.where(here, jnp.where(first, gate[0], gate[1]), 0.0).T.astype(BF)
            rows = jnp.dot(table, XG[slot, 0:TOK, :], preferred_element_type=F32).astype(BF)
            XD[0, s * CAP : (s + 1) * CAP, :] = rows[0:CAP]
            XD[1, s * CAP : (s + 1) * CAP, :] = rows[CAP : 2 * CAP]
        for j in range(2):
            gu = jnp.dot(XD[j], W1[j].reshape(D, 2 * FFE), preferred_element_type=F32)
            g, u = gu[:, :FFE], gu[:, FFE:]
            act = (g / (1.0 + jnp.exp(-g)) * u).astype(BF)
            res = jnp.dot(act, W2[j].reshape(FFE, D), preferred_element_type=F32).astype(BF)
            for s in range(4):
                Y[s, j * CAP : (j + 1) * CAP, :] = res[s * CAP : (s + 1) * CAP]
        for s, (rel_c, rel_z) in enumerate(sources):
            part = jnp.dot(CM[s], Y[s], preferred_element_type=F32)
            if rel_c == 0:
                PF[n * 2 + rel_z] = part
            else:
                CS[n * 2 + rel_z] = part.astype(BF)
                chunk_copy(n * 2 + rel_z).start()

    def summed(n, r):
        cp.arrived(CR.at[2 * n + r], s_c + 2 * n + r)
        return PF[2 * n + r] + CR[2 * n + r].astype(F32)

    def reduce_far():
        for r in (1, 0):
            S1S[r] = summed(0, r).astype(BF)
            for i in range(2):
                cut = pl.ds(64 * i, 64)
                cp.start(
                    S1S.at[r, cut],
                    S1R.at[r, cut],
                    s_1[r][i],
                    sides[i],
                    functools.partial(lambda r, i: S1S.at[r, pl.ds(64 * i, 64)], r, i),
                )

    def reduce_side(i):
        for r in (1, 0):
            part = summed(1 + i, r)
            cut = pl.ds(64 * i, 64)
            cp.arrived(S1R.at[r, cut], s_1[r][i])
            S2S[i, r] = part.astype(BF)
            S2S[i, r, cut, :] = (part[64 * i : 64 * i + 64] + S1R[r, cut, :].astype(F32)).astype(BF)
            cp.start(
                S2S.at[i, r],
                S2R.at[i, r],
                s_2[i][r],
                sides[i],
                functools.partial(lambda i, r: S2S.at[i, r], i, r),
            )

    @pl.loop(0, 4)
    def _(n):
        chunk(n)

        @pl.when(n == 1)
        def _():
            reduce_far()

        @pl.when(n == 2)
        def _():
            reduce_side(0)

        @pl.when(n == 3)
        def _():
            reduce_side(1)

    for r in (1, 0):
        part = summed(3, r)
        for i in range(2):
            cp.arrived(S2R.at[i, r], s_2[i][r])
            part += S2R[i, r].astype(F32)
        if r == 1:
            ZS[...] = part.astype(BF)
            cp.start(ZS, ZR, s_z, beside)
    cp.arrived(ZR, s_z)
    out[...] = (HID[...] + part + ZR[...].astype(F32)).astype(BF)

    for n in range(8):
        chunk_copy(n).wait_send()
    w_drain()
    cp.drain()


def per_device(
    resid, queries, suffix_kv, prefix_kv, segments, o_weight, norm_gain, router, routes, w_gate_up, w_down
):
    vm = pl.BlockSpec(memory_space=pltpu.VMEM)
    hbm = pl.BlockSpec(memory_space=pl.ANY)
    args = (
        resid,
        queries,
        suffix_kv.reshape(TOK, 1024),
        prefix_kv.reshape(64, 1024),
        segments,
        segments.reshape(TOK, 1),
        jnp.pad(o_weight, ((0, 2), (0, 0))),
        jnp.asarray(spread_matrix(), BF),
        norm_gain.reshape(1, D),
        router.T,
        routes.T,
        w_gate_up.reshape(2, 96, 1024),
        w_down.reshape(64, D),
    )
    specs = [vm, vm, vm, hbm, vm, vm, hbm, vm, vm, vm, vm, hbm, hbm]
    return pl.pallas_call(
        kernel,
        out_shape=jax.ShapeDtypeStruct((TOK, D), BF),
        in_specs=specs,
        out_specs=vm,
        scratch_shapes=[
            pltpu.VMEM((32, 64, 1024), BF),
            pltpu.VMEM((4, 2, 4, 8, 8, D), BF),
            pltpu.VMEM((2, 4, 2, 2, 96, 1024), BF),
            pltpu.VMEM((2, 4, 2, 64, D), BF),
            pltpu.VMEM((16, ROWS, D), BF),
            pltpu.VMEM((8, 384, 128), BF),
            pltpu.VMEM((8, 384, 128), F32),
            pltpu.VMEM((4, TOK, 512), BF),
            pltpu.VMEM((384, TOK), F32),
            pltpu.VMEM((TOK, D), F32),
            pltpu.VMEM((2, 4 * CAP, D), BF),
            pltpu.VMEM((4, TOK, D), BF),
            pltpu.VMEM((4, TOK, TOK), BF),
            pltpu.VMEM((8, TOK, D), F32),
            pltpu.VMEM((8, TOK, D), BF),
            pltpu.VMEM((8, TOK, D), BF),
            pltpu.VMEM((2, TOK, D), BF),
            pltpu.VMEM((2, TOK, D), BF),
            pltpu.VMEM((2, 2, TOK, D), BF),
            pltpu.VMEM((2, 2, TOK, D), BF),
            pltpu.VMEM((TOK, D), BF),
            pltpu.VMEM((TOK, D), BF),
            pltpu.SemaphoreType.DMA((192,)),
            pltpu.SemaphoreType.DMA((192,)),
            pltpu.SemaphoreType.DMA((2,)),
        ],
        compiler_params=pltpu.CompilerParams(
            collective_id=0, has_side_effects=True, vmem_limit_bytes=67043328
        ),
    )(*args)


def solution(mesh):
    return jax.shard_map(
        per_device,
        mesh=mesh,
        in_specs=(
            P(("grp", "dev"), None),
            P(("grp", "dev"), None),
            P(("grp", "dev"), None, None),
            P("grp", "dev", None, None),
            P(("grp", "dev"), None),
            P(("grp", "dev"), None),
            P(),
            P(),
            P(("grp", "dev"), None),
            P("dev", "grp", None),
            P("dev", "grp", None),
        ),
        out_specs=P(("grp", "dev"), None),
        check_vma=False,
    )
```

```python
import functools

import jax
import jax.numpy as jnp
import numpy as np
from jax import lax
from jax.experimental import pallas as pl
from jax.experimental.pallas import tpu as pltpu
from jax.sharding import PartitionSpec as P

D = 1536
KVH = 8
FFE = 512
CAP = 48
EXPERTS = 32
TOK = 128
ROWS = 144
BF = jnp.bfloat16
F32 = jnp.float32
MESH = pl.DeviceIdType.MESH


def spread_matrix():
    out = np.zeros((384, 512), np.float32)
    for q in range(512):
        i, z, x, c = q % 8, (q // 8) % 8, (q // 64) % 4, q // 256
        if i < 6:
            out[((z % 2) * 32 + x * 8 + (z // 2) * 2 + c) * 6 + i, q] = 1.0
    return out


class Copies:
    def __init__(self, send, recv):
        self.send, self.recv, self.sends, self.recvs, self.open = send, recv, 0, 0, []

    def slot(self):
        self.recvs += 1
        return self.recvs - 1

    def start(self, src, dst, slot, device, again=None):
        copy = pltpu.make_async_remote_copy(
            src_ref=src,
            dst_ref=dst,
            send_sem=self.send.at[self.sends],
            recv_sem=self.recv.at[slot],
            device_id=device,
            device_id_type=MESH,
        )
        self.open.append((self.sends, again or (lambda: src)))
        self.sends += 1
        copy.start()

    def arrived(self, ref, slot):
        pltpu.make_async_copy(ref, ref, self.recv.at[slot]).wait()

    def drain(self):
        for index, source in self.open:
            ref = source()
            pltpu.make_async_copy(ref, ref, self.send.at[index]).wait()


def kernel(
    resid,
    queries,
    suffix,
    kv_own,
    seg_row,
    o_own,
    spread,
    gain,
    router_t,
    routes,
    w1_own,
    w2_own,
    out,
    KV,
    O,
    W1,
    W2,
    XG,
    QH,
    OH,
    AP,
    MK,
    HID,
    XD,
    Y,
    CM,
    PF,
    CS,
    CR,
    S1S,
    S1R,
    S2S,
    S2R,
    ZS,
    ZR,
    send_sem,
    recv_sem,
    local_sem,
):
    grp, dev = lax.axis_index("grp"), lax.axis_index("dev")
    y, zl = lax.div(grp, 2), lax.rem(grp, 2)
    x, zh, c = lax.div(dev, 8), lax.rem(lax.div(dev, 2), 4), lax.rem(dev, 2)

    def at(x_=x, y_=y, zh_=zh, zl_=zl, c_=c):
        return (y_ * 2 + zl_, x_ * 8 + zh_ * 2 + c_)

    def up(v, k=1):
        return lax.rem(v + k, 4)

    right, left, partner = at(x_=up(x)), at(x_=up(x, 3)), at(c_=1 - c)
    sides = (right, left)
    y_sides = (at(y_=up(y)), at(y_=up(y, 3)))
    beside = at(zl_=1 - zl)

    barrier = pltpu.get_barrier_semaphore()
    friends = [right, left, partner, y_sides[0], y_sides[1], at(y_=up(y, 2)), beside]
    for k in (1, 2, 3):
        friends += [at(zh_=up(zh, k)), at(zh_=up(zh, k), zl_=1 - zl)]
    for friend in friends:
        pl.semaphore_signal(barrier, inc=1, device_id=friend, device_id_type=MESH)
    pl.semaphore_wait(barrier, len(friends))

    cp = Copies(send_sem, recv_sem)

    def kv_slot(x_, zh_, c_=c):
        return x_ * 8 + zh_ * 2 + c_

    kv_z = [None] + [cp.slot() for _ in range(3)]
    kv_x = [[cp.slot() for _ in range(2)] for _ in range(4)]
    kv_half = [[cp.slot() for _ in range(2)] for _ in range(4)]
    kv_p = [[cp.slot() for _ in range(4)] for _ in range(4)]
    o_z = [[cp.slot() for _ in range(2)] for _ in range(4)]
    o_y = [None] + [cp.slot() for _ in range(3)]
    o_x = [cp.slot() for _ in range(2)]
    o_half = [cp.slot() for _ in range(2)]
    o_p = [cp.slot() for _ in range(4)]
    w_z = [[[cp.slot() for _ in range(3)] for _ in range(2)] for _ in range(2)]
    w_y = [[[cp.slot() for _ in range(3)] for _ in range(2)] for _ in range(2)]
    w_half = [[[cp.slot() for _ in range(3)] for _ in range(2)] for _ in range(2)]
    t_zl = cp.slot()
    t_x = [[cp.slot() for _ in range(2)] for _ in range(2)]
    t_half = [[cp.slot() for _ in range(2)] for _ in range(2)]
    t_p = [[cp.slot() for _ in range(4)] for _ in range(2)]
    s_c = cp.recvs
    for _ in range(8):
        cp.slot()
    s_1 = [[cp.slot() for _ in range(2)] for _ in range(2)]
    s_2 = [[cp.slot() for _ in range(2)] for _ in range(2)]
    s_z = cp.slot()

    mine = KV.at[kv_slot(x, zh)]
    local_kv = pltpu.make_async_copy(kv_own, mine, local_sem.at[0])
    local_kv.start()
    for k in (1, 2, 3):
        cp.start(kv_own, mine, kv_z[k], at(zh_=up(zh, k)))
    for i in range(2):
        cp.start(kv_own, mine, kv_x[0][i], sides[i])
    cp.start(kv_own, mine, kv_p[0][0], partner)

    my_z = zh * 2 + zl
    o_mine = O.at[y, c, x, my_z]
    local_o = pltpu.make_async_copy(o_own, o_mine, local_sem.at[1])
    local_o.start()
    for k in range(4):
        for j in range(2):
            if k or j:
                cp.start(o_own, o_mine, o_z[k][j], at(zh_=up(zh, k), zl_=zl if j == 0 else 1 - zl))

    pieces = (
        lambda j, y_, z_: W1.at[j, y_, z_, 0],
        lambda j, y_, z_: W1.at[j, y_, z_, 1],
        lambda j, y_, z_: W2.at[j, y_, z_],
    )
    own_pieces = (w1_own.at[0], w1_own.at[1], w2_own)
    w_target = lax.div(zh, 2)
    w_started = []

    def w_start(n):
        for j in range(2):
            for z_ in range(2):

                @pl.when((lax.rem(zh, 2) == j) & (zl == z_))
                def _():
                    for k in range(4):
                        sem = send_sem.at[cp.sends + k]
                        copy = pltpu.make_async_remote_copy(
                            src_ref=own_pieces[n],
                            dst_ref=pieces[n](j, y, z_),
                            send_sem=sem,
                            recv_sem=recv_sem.at[w_z[j][z_][n]],
                            device_id=at(zh_=up(zh, k), zl_=w_target),
                            device_id_type=MESH,
                        )
                        if k:
                            copy.start()
                        else:

                            @pl.when(w_target != zl)
                            def _():
                                copy.start()

                            @pl.when(w_target == zl)
                            def _():
                                pltpu.make_async_copy(
                                    own_pieces[n], pieces[n](j, y, z_), recv_sem.at[w_z[j][z_][n]]
                                ).start()

        w_started.append((n, cp.sends))
        cp.sends += 4

    def w_drain():
        for n, first in w_started:
            for k in range(4):
                copy = pltpu.make_async_remote_copy(
                    src_ref=own_pieces[n],
                    dst_ref=pieces[n](0, y, 0),
                    send_sem=send_sem.at[first + k],
                    recv_sem=recv_sem.at[w_z[0][0][n]],
                    device_id=at(zh_=up(zh, k), zl_=w_target),
                    device_id_type=MESH,
                )
                if k:
                    copy.wait_send()
                else:

                    @pl.when(w_target != zl)
                    def _():
                        copy.wait_send()

    def w_along_y(n):
        for j in range(2):
            for z_ in range(2):
                cp.arrived(pieces[n](j, y, z_), w_z[j][z_][n])
            both = pieces[n](j, y, slice(None))
            for i in range(2):
                cp.start(both, both, w_y[j][i][n], y_sides[i])

    def w_forward(n):
        for j in range(2):
            for i in range(2):
                origin = up(y, 3) if i == 0 else up(y)
                cp.arrived(pieces[n](j, origin, slice(None)), w_y[j][i][n])
                half = pieces[n](j, origin, i)
                cp.start(half, half, w_half[j][i][n], y_sides[i])

    def w_finish(n):
        for j in range(2):
            for i in range(2):
                cp.arrived(pieces[n](j, up(y, 2), i), w_half[j][i][n])

    for n in range(3):
        w_start(n)

    lane = lax.broadcasted_iota(jnp.int32, (TOK, 128), 1)
    low = lane < 64
    for p in range(4):
        tiles = [queries[:, p * 384 + 128 * i : p * 384 + 128 * (i + 1)].astype(F32) * 0.125 for i in range(3)]
        turned = [pltpu.roll(t, 64, 1) for t in (tiles[0], tiles[2])]
        heads = (
            jnp.where(low, tiles[0], 0.0),
            jnp.where(low, turned[0], 0.0),
            jnp.where(low, tiles[1], 0.0),
            jnp.where(low, 0.0, tiles[1]),
            jnp.where(low, 0.0, turned[1]),
            jnp.where(low, 0.0, tiles[2]),
        )
        for h in range(6):
            QH[2 * p + h // 3, (h % 3) * 128 : (h % 3 + 1) * 128, :] = heads[h].astype(BF)
    row = lax.broadcasted_iota(jnp.int32, (TOK, TOK), 0)
    col = lax.broadcasted_iota(jnp.int32, (TOK, TOK), 1)
    seg = jnp.broadcast_to(seg_row[...].astype(F32), (TOK, TOK))
    allowed = (seg == seg.T) & (col <= row)
    bias = jnp.where(allowed, 0.0, -1e30)
    for i in range(3):
        MK[i * 128 : (i + 1) * 128, :] = bias

    for k in (1, 2, 3):
        piece = KV.at[kv_slot(x, up(zh, 4 - k))]
        cp.arrived(piece, kv_z[k])
        for i in range(2):
            cp.start(piece, piece, kv_x[k][i], sides[i])
        cp.start(piece, piece, kv_p[k][0], partner)
    for k in range(4):
        for i in range(2):
            slot = kv_slot(up(x, 3) if i == 0 else up(x), up(zh, 4 - k))
            piece = KV.at[slot]
            cp.arrived(piece, kv_x[k][i])
            half = KV.at[slot, 32 * i : 32 * (i + 1)]
            cp.start(half, half, kv_half[k][i], sides[i])
            cp.start(piece, piece, kv_p[k][1 + i], partner)
    local_o.wait()
    for k in range(4):
        for j in range(2):
            if k or j:
                zz = up(zh, 4 - k) * 2 + (zl if j == 0 else 1 - zl)
                cp.arrived(O.at[y, c, x, zz], o_z[k][j])
    for k in (1, 2, 3):
        cp.start(O.at[y, c, x], O.at[y, c, x], o_y[k], at(y_=up(y, k)))
    w_along_y(0)
    for k in range(4):
        slot = kv_slot(up(x, 2), up(zh, 4 - k))
        for i in range(2):
            cp.arrived(KV.at[slot, 32 * i : 32 * (i + 1)], kv_half[k][i])
        cp.start(KV.at[slot], KV.at[slot], kv_p[k][3], partner)
    for k in (1, 2, 3):
        cp.arrived(O.at[up(y, 4 - k), c, x], o_y[k])
    for i in range(2):
        cp.start(O.at[:, c, x], O.at[:, c, x], o_x[i], sides[i])
    cp.start(O.at[:, c, x], O.at[:, c, x], o_p[0], partner)
    w_along_y(1)
    for k in range(4):
        for i, from_x in enumerate((x, up(x, 3), up(x), up(x, 2))):
            cp.arrived(KV.at[kv_slot(from_x, up(zh, 4 - k), 1 - c)], kv_p[k][i])
    local_kv.wait()

    nt = (((1,), (1,)), ((), ()))

    def attend(h):
        p = lax.div(h, 2)
        k_cols = pl.ds(pl.multiple_of(p * 128, 128), 128)
        v_cols = pl.ds(pl.multiple_of(512 + p * 128, 128), 128)
        q = QH[h]
        s1 = lax.dot_general(q, KV[:, :, k_cols].reshape(2048, 128), nt, preferred_element_type=F32)
        s2 = lax.dot_general(q, suffix[:, k_cols], nt, preferred_element_type=F32) + MK[...]
        top = jnp.maximum(jnp.max(s1, axis=1, keepdims=True), jnp.max(s2, axis=1, keepdims=True))
        p1, p2 = jnp.exp(s1 - top), jnp.exp(s2 - top)
        total = jnp.sum(p1, axis=1, keepdims=True) + jnp.sum(p2, axis=1, keepdims=True)
        acc = jnp.dot(p1.astype(BF), KV[:, :, v_cols].reshape(2048, 128), preferred_element_type=F32)
        acc += jnp.dot(p2.astype(BF), suffix[:, v_cols], preferred_element_type=F32)
        OH[h] = acc / total

    @pl.loop(0, 4)
    def _(h):
        attend(h)

    for i in range(2):
        origin = up(x, 3) if i == 0 else up(x)
        cp.arrived(O.at[:, c, origin], o_x[i])
        half = O.at[pl.ds(2 * i, 2), c, origin]
        cp.start(half, half, o_half[i], sides[i])
        cp.start(O.at[:, c, origin], O.at[:, c, origin], o_p[1 + i], partner)

    w_along_y(2)

    @pl.loop(4, 8)
    def _(h):
        attend(h)

    w_forward(0)

    for p in range(4):
        a = [OH[2 * p + h // 3, (h % 3) * 128 : (h % 3 + 1) * 128, :] for h in range(6)]
        tiles = (
            jnp.where(low, a[0], pltpu.roll(a[1], 64, 1)),
            jnp.where(low, a[2], a[3]),
            jnp.where(low, pltpu.roll(a[4], 64, 1), a[5]),
        )
        att = jnp.concatenate([t.astype(BF) for t in tiles], axis=1)
        AP[p] = jnp.dot(att, spread[...], preferred_element_type=F32).astype(BF)

    far = up(x, 2)
    for i in range(2):
        cp.arrived(O.at[pl.ds(2 * i, 2), c, far], o_half[i])
    cp.start(O.at[:, c, far], O.at[:, c, far], o_p[3], partner)
    for i, from_x in enumerate((x, up(x, 3), up(x), far)):
        cp.arrived(O.at[:, 1 - c, from_x], o_p[i])

    total = resid[...].astype(F32)
    for p in range(4):
        total += jnp.dot(AP[p], O[p].reshape(512, D), preferred_element_type=F32)
    HID[...] = total
    scale = lax.rsqrt(jnp.mean(total * total, axis=1, keepdims=True) + 1e-06)
    normed = (total * scale * gain[...]).astype(BF)
    logits = lax.dot_general(router_t[...], normed, nt, preferred_element_type=F32)
    routes_t = routes[...].astype(F32).T
    expert = lax.broadcasted_iota(jnp.int32, (EXPERTS, TOK), 0).astype(F32)
    chosen = routes_t[0:1, :] == expert
    for k in range(1, 8):
        chosen = chosen | (routes_t[k : k + 1, :] == expert)
    sig = jnp.where(chosen, 1.0 / (1.0 + jnp.exp(-logits)), 0.0)
    gates = sig / jnp.sum(sig, axis=0, keepdims=True)
    upper = jnp.where(row <= col, 1.0, 0.0).astype(BF)
    hit = jnp.where(chosen, 1.0, 0.0)
    rank = jnp.dot(hit.astype(BF), upper, preferred_element_type=F32)
    rank = jnp.where(chosen, rank - 1.0, -1.0)

    def tok(x_, z_, c_=c):
        return (c_ * 4 + x_) * 2 + z_

    own = tok(x, zl)
    XG[own, 0:TOK, :] = normed
    for n in range(4):
        XG[own, TOK : TOK + 16, 128 * n : 128 * (n + 1)] = jnp.concatenate(
            [gates[8 * n : 8 * n + 8], rank[8 * n : 8 * n + 8]], axis=0
        ).astype(BF)
    cp.start(XG.at[own], XG.at[own], t_zl, beside)
    for i in range(2):
        cp.start(XG.at[own], XG.at[own], t_x[0][i], sides[i])
    cp.start(XG.at[own], XG.at[own], t_p[0][0], partner)
    piece = XG.at[tok(x, 1 - zl)]
    cp.arrived(piece, t_zl)
    for i in range(2):
        cp.start(piece, piece, t_x[1][i], sides[i])
    cp.start(piece, piece, t_p[1][0], partner)
    w_forward(1)
    cuts = ((0, 64), (64, ROWS - 64))
    for r in range(2):
        z_ = zl if r == 0 else 1 - zl
        for i in range(2):
            slot = tok(up(x, 3) if i == 0 else up(x), z_)
            cp.arrived(XG.at[slot], t_x[r][i])
            half = XG.at[slot, pl.ds(*cuts[i])]
            cp.start(half, half, t_half[r][i], sides[i])
            cp.start(XG.at[slot], XG.at[slot], t_p[r][1 + i], partner)
    w_forward(2)
    for r in range(2):
        z_ = zl if r == 0 else 1 - zl
        slot = tok(far, z_)
        for i in range(2):
            cp.arrived(XG.at[slot, pl.ds(*cuts[i])], t_half[r][i])
        cp.start(XG.at[slot], XG.at[slot], t_p[r][3], partner)
    for r in range(2):
        z_ = zl if r == 0 else 1 - zl
        for i, from_x in enumerate((x, up(x, 3), up(x), far)):
            cp.arrived(XG.at[tok(from_x, z_, 1 - c)], t_p[r][i])
    for n in range(3):
        w_finish(n)

    e_cols = pl.ds(pl.multiple_of(x * 128, 128), 128)
    slot_row = lax.broadcasted_iota(jnp.int32, (TOK, TOK), 0)
    slot_f = jnp.where(slot_row < CAP, slot_row, slot_row - CAP).astype(F32)
    first = slot_row < CAP
    sub = lax.broadcasted_iota(jnp.int32, (8, TOK), 0)
    picks = [sub == (2 * zl + j) * 2 + c for j in range(2)]
    sources = [(rel_c, rel_z) for rel_c in range(2) for rel_z in range(2)]
    Y[...] = jnp.zeros_like(Y)

    first_c = cp.sends
    cp.sends += 8

    def chunk_copy(n):
        return pltpu.make_async_remote_copy(
            src_ref=CS.at[n],
            dst_ref=CR.at[n],
            send_sem=send_sem.at[first_c + n],
            recv_sem=recv_sem.at[s_c + n],
            device_id=partner,
            device_id_type=MESH,
        )

    def chunk(n):
        from_x = lax.rem(x + 2 - n + 3 * lax.div(n, 2) - 2 * lax.div(n, 3), 4)
        for s, (rel_c, rel_z) in enumerate(sources):
            slot = tok(from_x, lax.rem(zl + rel_z, 2), lax.rem(c + rel_c, 2))
            info = XG[slot, TOK : TOK + 16, e_cols].astype(F32)
            gate, rank = [
                [jnp.sum(jnp.where(pick, part, 0.0), axis=0, keepdims=True) for pick in picks]
                for part in (info[0:8], info[8:16])
            ]
            here = jnp.where(first, rank[0], rank[1]) == slot_f
            table = jnp.where(here, 1.0, 0.0).astype(BF)
            CM[s] = jnp.where(here, jnp.where(first, gate[0], gate[1]), 0.0).T.astype(BF)
            rows = jnp.dot(table, XG[slot, 0:TOK, :], preferred_element_type=F32).astype(BF)
            XD[0, s * CAP : (s + 1) * CAP, :] = rows[0:CAP]
            XD[1, s * CAP : (s + 1) * CAP, :] = rows[CAP : 2 * CAP]
        for j in range(2):
            gu = jnp.dot(XD[j], W1[j].reshape(D, 2 * FFE), preferred_element_type=F32)
            g, u = gu[:, :FFE], gu[:, FFE:]
            act = (g / (1.0 + jnp.exp(-g)) * u).astype(BF)
            res = jnp.dot(act, W2[j].reshape(FFE, D), preferred_element_type=F32).astype(BF)
            for s in range(4):
                Y[s, j * CAP : (j + 1) * CAP, :] = res[s * CAP : (s + 1) * CAP]
        for s, (rel_c, rel_z) in enumerate(sources):
            part = jnp.dot(CM[s], Y[s], preferred_element_type=F32)
            if rel_c == 0:
                PF[n * 2 + rel_z] = part
            else:
                CS[n * 2 + rel_z] = part.astype(BF)
                chunk_copy(n * 2 + rel_z).start()

    def summed(n, r):
        cp.arrived(CR.at[2 * n + r], s_c + 2 * n + r)
        return PF[2 * n + r] + CR[2 * n + r].astype(F32)

    def reduce_far():
        for r in (1, 0):
            S1S[r] = summed(0, r).astype(BF)
            for i in range(2):
                cut = pl.ds(64 * i, 64)
                cp.start(
                    S1S.at[r, cut],
                    S1R.at[r, cut],
                    s_1[r][i],
                    sides[i],
                    functools.partial(lambda r, i: S1S.at[r, pl.ds(64 * i, 64)], r, i),
                )

    def reduce_side(i):
        for r in (1, 0):
            part = summed(1 + i, r)
            cut = pl.ds(64 * i, 64)
            cp.arrived(S1R.at[r, cut], s_1[r][i])
            S2S[i, r] = part.astype(BF)
            S2S[i, r, cut, :] = (part[64 * i : 64 * i + 64] + S1R[r, cut, :].astype(F32)).astype(BF)
            cp.start(
                S2S.at[i, r],
                S2R.at[i, r],
                s_2[i][r],
                sides[i],
                functools.partial(lambda i, r: S2S.at[i, r], i, r),
            )

    @pl.loop(0, 4)
    def _(n):
        chunk(n)

        @pl.when(n == 1)
        def _():
            reduce_far()

        @pl.when(n == 2)
        def _():
            reduce_side(0)

        @pl.when(n == 3)
        def _():
            reduce_side(1)

    for r in (1, 0):
        part = summed(3, r)
        for i in range(2):
            cp.arrived(S2R.at[i, r], s_2[i][r])
            part += S2R[i, r].astype(F32)
        if r == 1:
            ZS[...] = part.astype(BF)
            cp.start(ZS, ZR, s_z, beside)
    cp.arrived(ZR, s_z)
    out[...] = (HID[...] + part + ZR[...].astype(F32)).astype(BF)

    for n in range(8):
        chunk_copy(n).wait_send()
    w_drain()
    cp.drain()


def per_device(
    resid, queries, suffix_kv, prefix_kv, segments, o_weight, norm_gain, router, routes, w_gate_up, w_down
):
    vm = pl.BlockSpec(memory_space=pltpu.VMEM)
    hbm = pl.BlockSpec(memory_space=pl.ANY)
    args = (
        resid,
        queries,
        suffix_kv.reshape(TOK, 1024),
        prefix_kv.reshape(64, 1024),
        segments,
        jnp.pad(o_weight, ((0, 2), (0, 0))),
        jnp.asarray(spread_matrix(), BF),
        norm_gain.reshape(1, D),
        router.T,
        routes,
        w_gate_up.reshape(2, 96, 1024),
        w_down.reshape(64, D),
    )
    specs = [vm, vm, vm, hbm, vm, hbm, vm, vm, vm, vm, hbm, hbm]
    return pl.pallas_call(
        kernel,
        out_shape=jax.ShapeDtypeStruct((TOK, D), BF),
        in_specs=specs,
        out_specs=vm,
        scratch_shapes=[
            pltpu.VMEM((32, 64, 1024), BF),
            pltpu.VMEM((4, 2, 4, 8, 8, D), BF),
            pltpu.VMEM((2, 4, 2, 2, 96, 1024), BF),
            pltpu.VMEM((2, 4, 2, 64, D), BF),
            pltpu.VMEM((16, ROWS, D), BF),
            pltpu.VMEM((8, 384, 128), BF),
            pltpu.VMEM((8, 384, 128), F32),
            pltpu.VMEM((4, TOK, 512), BF),
            pltpu.VMEM((384, TOK), F32),
            pltpu.VMEM((TOK, D), F32),
            pltpu.VMEM((2, 4 * CAP, D), BF),
            pltpu.VMEM((4, TOK, D), BF),
            pltpu.VMEM((4, TOK, TOK), BF),
            pltpu.VMEM((8, TOK, D), F32),
            pltpu.VMEM((8, TOK, D), BF),
            pltpu.VMEM((8, TOK, D), BF),
            pltpu.VMEM((2, TOK, D), BF),
            pltpu.VMEM((2, TOK, D), BF),
            pltpu.VMEM((2, 2, TOK, D), BF),
            pltpu.VMEM((2, 2, TOK, D), BF),
            pltpu.VMEM((TOK, D), BF),
            pltpu.VMEM((TOK, D), BF),
            pltpu.SemaphoreType.DMA((192,)),
            pltpu.SemaphoreType.DMA((192,)),
            pltpu.SemaphoreType.DMA((2,)),
        ],
        compiler_params=pltpu.CompilerParams(
            collective_id=0, has_side_effects=True, vmem_limit_bytes=67043328
        ),
    )(*args)


def solution(mesh):
    return jax.shard_map(
        per_device,
        mesh=mesh,
        in_specs=(
            P(("grp", "dev"), None),
            P(("grp", "dev"), None),
            P(("grp", "dev"), None, None),
            P("grp", "dev", None, None),
            P(("grp", "dev"), None),
            P(("grp", "dev"), None),
            P(),
            P(),
            P(("grp", "dev"), None),
            P("dev", "grp", None),
            P("dev", "grp", None),
        ),
        out_specs=P(("grp", "dev"), None),
        check_vma=False,
    )
```
